256 devices in a mesh: row: 32 (over x_hi, z, core), col: 8 (over y, x_lo).
Axes of the slice: x: 4 (x_hi: 2, x_lo: 2; x = x_hi * 2 + x_lo), y: 4, z: 8, core: 2. Of those that a mesh axis runs over, the one named last changes fastest.
Arguments:
- x_tiles: bfloat16 [64, 32, 1, 128, 128], P('row', 'col'), may hold values from -0.5390625 to 0.5390625
- x_cols: int32 [64, 32, 1], P('row', 'col'), may hold values from 0 to 1, as said below
- keep_cols: int32 [64, 32, 2], P('row', 'col'), may hold values from 0 to 1, as said below
Outputs:
- square: bfloat16 [64, 32, 2, 128, 128], P('row', 'col')
- purified: bfloat16 [64, 32, 2, 128, 128], P('row', 'col')
The draws below stay inside these ranges and needn't reach their ends.
Inputs may be any that keep to these rules, and one draw needn't show every extreme that they name: `x_cols`: within each block row and column panel the 1 entries are distinct. `keep_cols`: within each block row and column panel the 2 entries are distinct.
All inputs are finite; a program needn't handle non-finite values.
Results may differ from the reference program's by a relative error of at most 0.0049.
Values may be sent and summed in bfloat16 or wider, within the bound.
A program may use at most 64 MiB of HBM per device.

```python
import jax
import jax.numpy as jnp
from jax import lax

TILE = 128
BR = 2
KP = 1
K2 = 2
NB = 64
NPAN = 32


def draw_x_cols(key, part):
    keys = jax.random.split(jax.random.fold_in(key, 11), NB * NPAN)
    picks = jax.vmap(lambda single: jax.random.permutation(single, BR)[:KP])(keys)
    return picks.reshape(NB, NPAN, KP).astype(jnp.int32)


def draw_keep_cols(key, part):
    keys = jax.random.split(jax.random.fold_in(key, 23), NB * NPAN)
    picks = jax.vmap(lambda single: jax.random.permutation(single, BR)[:K2])(keys)
    return picks.reshape(NB, NPAN, K2).astype(jnp.int32)


def levels(rng, extent, shards, smallest, top_value):
    gain, own = 1.0, jax.random.fold_in(rng, 6)
    for position, blocks in shards:
        heights = jnp.exp(jax.random.uniform(jax.random.fold_in(own, position), (blocks,), jnp.float32, smallest / len(shards), top_value / len(shards)))
        gain = gain * jnp.repeat(heights, extent[position] // blocks).reshape([-1 if axis == position else 1 for axis in range(len(extent))])
    return gain


def noise(stream_key, shape, width, reach, cuts=(), kind=jnp.bfloat16):
    result = width * jax.random.normal(stream_key, shape, jnp.float32)
    if cuts:
        result = result * levels(stream_key, shape, cuts, -0.22, 0.18)
    return jnp.clip(result, -reach, reach).astype(kind)


def setup_inputs(seed: int = 0) -> dict:
    key_of = jax.random.split(jax.random.key(seed), 4)
    return {
        "x_tiles": noise(key_of[0], (NB, NPAN, KP, TILE, TILE), 0.09, 0.5390625, ((0, 32), (1, 8))),
        "x_cols": draw_x_cols(jax.random.fold_in(key_of[3], 71), 0),
        "keep_cols": draw_keep_cols(jax.random.fold_in(key_of[3], 71), 0),
    }


def row_product(a_tiles, a_cols, kept_cols, x_tiles, x_cols):
    panels = a_cols.shape[0]
    rows_b = (jnp.arange(panels, dtype=jnp.int32)[:, None] * BR + a_cols).astype(jnp.int32)
    b_rows = x_tiles[rows_b].astype(jnp.float32)
    b_cols = x_cols[rows_b]
    matched = (b_cols[:, :, :, None, :] == kept_cols[None, None, :, :, None]).astype(jnp.float32)
    selected = jnp.einsum('paqtb,paqbnk->paqtnk', matched, b_rows)
    return jnp.einsum('pamn,paqtnk->qtmk', a_tiles.astype(jnp.float32), selected)


def reference(x_tiles, x_cols, keep_cols):
    indices = jnp.arange(NB, dtype=jnp.int32)

    def square_row(index):
        return row_product(x_tiles[index], x_cols[index], keep_cols[index], x_tiles, x_cols)

    square = lax.map(square_row, indices).astype(jnp.bfloat16)

    def cube_row(index):
        return row_product(square[index], keep_cols[index], keep_cols[index], x_tiles, x_cols)

    cube = lax.map(cube_row, indices)
    purified = (3.0 * square.astype(jnp.float32) - 2.0 * cube).astype(jnp.bfloat16)
    return square, purified
```

```python
import functools

import jax
import jax.numpy as jnp
from jax import lax
from jax.experimental import pallas as pl
from jax.experimental.pallas import tpu as pltpu
from jax.sharding import PartitionSpec as P

T = 128
HEAD = 16
ROWS = HEAD + 8 * T
NP = 4
BF = jnp.bfloat16
F32 = jnp.float32


def span(panel):
    return (0, HEAD + 2 * T) if panel == 0 else (HEAD + 2 * T * panel, 2 * T)


def half_span(panel, which):
    first, size = span(panel)
    cut = size - T
    return (first, cut) if which == 0 else (first + cut, T)


A_HALF = ((0, HEAD + 4 * T), (HEAD + 4 * T, 4 * T))


def kernel(
    x_hbm, xc, kc, sq_hbm, pu_hbm,
    b_raw, bd, a_raw, a_dense, s_buf, acc, part, sq_v, pu_v,
    load_sem, xh_s, xh_r, z_s, z_r, core_s, core_r,
    a_s, ax_r, ay_r, s_s, sx_r, sy_r, out_sem,
):
    row = lax.axis_index("row")
    me_c = lax.axis_index("col")
    xhi, z, core = row // 16, (row // 2) % 8, row % 2
    y, xlo = me_c // 2, me_c % 2

    def row_of(a, b, c):
        return (a * 8 + b) * 2 + c

    z_peer = (row_of(xhi, (z + 1) % 8, core), row_of(xhi, (z + 7) % 8, core))
    xh_peer = row_of(1 - xhi, z, core)
    core_peer = row_of(xhi, z, 1 - core)
    y_peer = (((y + 1) % 4) * 2 + xlo, ((y + 3) % 4) * 2 + xlo)
    xl_peer = y * 2 + 1 - xlo

    own_b = b_raw.at[core, z, xhi]
    own_a = a_raw.at[me_c]
    loads = []
    for panel in range(NP):
        for i in range(2):
            rows = pl.ds(HEAD + 2 * T * panel + T * i, T)
            loads.append(pltpu.make_async_copy(x_hbm.at[i, panel, 0], own_b.at[rows], load_sem.at[0, panel, i]))
            loads.append(pltpu.make_async_copy(x_hbm.at[i, panel, 0], own_a.at[rows], load_sem.at[1, panel, i]))
    for copy in loads:
        copy.start()

    line = lax.broadcasted_iota(jnp.int32, (HEAD, T), 0)
    flags = jnp.zeros((HEAD, T), jnp.int32)
    for i in range(2):
        for panel in range(NP):
            flags = jnp.where(line == i * NP + panel, xc[i, panel, 0], flags)
    flags = flags.astype(F32).astype(BF)
    own_b[0:HEAD, :] = flags
    own_a[0:HEAD, :] = flags

    barrier = pltpu.get_barrier_semaphore()
    for peer in (z_peer[0], z_peer[1], xh_peer, core_peer):
        pl.semaphore_signal(barrier, inc=1, device_id={"row": peer}, device_id_type=pl.DeviceIdType.MESH)
    for peer in (y_peer[0], y_peer[1], xl_peer):
        pl.semaphore_signal(barrier, inc=1, device_id={"col": peer}, device_id_type=pl.DeviceIdType.MESH)
    pl.semaphore_wait(barrier, 7)
    for copy in loads:
        copy.wait()

    def remote(ref, send, recv, target):
        return pltpu.make_async_remote_copy(
            src_ref=ref, dst_ref=ref, send_sem=send, recv_sem=recv,
            device_id=target, device_id_type=pl.DeviceIdType.MESH,
        )

    def xh_copy(panel, plane):
        ref = b_raw.at[core, z, plane, pl.ds(*span(panel))]
        return remote(ref, xh_s, xh_r.at[panel], {"row": xh_peer})

    def z_copy(way, panel, hop, e, source):
        plane = xhi if e == 0 else 1 - xhi
        where = span(panel) if hop < 4 else half_span(panel, way)
        ref = b_raw.at[core, source, plane, pl.ds(*where)]
        return remote(ref, z_s.at[panel], z_r.at[way, panel, hop - 1, e], {"row": z_peer[way]})

    def behind(way, count):
        return (z + (8 - count if way == 0 else count)) % 8

    def z_send(way, panel, hop, e):
        z_copy(way, panel, hop, e, behind(way, hop - 1)).start()

    def z_wait(way, panel, hop, e):
        z_copy(way, panel, hop, e, behind(way, hop)).wait_recv()

    def core_send(panel, source, e, where):
        plane = xhi if e == 0 else 1 - xhi
        ref = b_raw.at[core, source, plane, pl.ds(*where)]
        remote(ref, core_s.at[panel], core_r.at[panel], {"row": core_peer}).start()

    def row_copy(buf, owner, where, send, recv, target):
        return remote(buf.at[owner, pl.ds(*where)], send, recv, {"col": target})

    class Gather:
        def __init__(self, buf, halves, send, x_recv, y_recv):
            self.buf, self.halves, self.send = buf, halves, send
            self.x_recv, self.y_recv = x_recv, y_recv
            self.total = halves[0][1] + halves[1][1]

        def owner(self, e, way, count):
            side = (y + (4 - count if way == 0 else count)) % 4
            return side * 2 + (xlo if e == 0 else 1 - xlo)

        def x_copy(self, owner):
            return row_copy(self.buf, owner, (0, self.total), self.send, self.x_recv, xl_peer)

        def y_copy(self, e, way, hop, which, owner):
            slot = which if hop == 1 else 2
            return row_copy(self.buf, owner, self.halves[which], self.send, self.y_recv.at[e, way, slot], y_peer[way])

        def send_y(self, e):
            for order in range(2):
                for way in range(2):
                    which = order if way == 0 else 1 - order
                    self.y_copy(e, way, 1, which, self.owner(e, way, 0)).start()

        def send_x(self):
            self.x_copy(me_c).start()

        def pass_x(self):
            self.x_copy(xl_peer).wait_recv()
            self.send_y(1)

        def pass_y(self, e):
            for way in range(2):
                self.y_copy(e, way, 1, way, self.owner(e, way, 1)).wait_recv()
                self.y_copy(e, way, 2, way, self.owner(e, way, 1)).start()

        def finish(self, e):
            for way in range(2):
                self.y_copy(e, way, 1, 1 - way, self.owner(e, way, 1)).wait_recv()
            for way in range(2):
                self.y_copy(e, way, 2, way, self.owner(e, way, 2)).wait_recv()

        def drain(self):
            done = self.buf.at[0:7]
            pltpu.make_async_copy(done, done, self.send).wait()

    a_g = Gather(a_raw, A_HALF, a_s, ax_r, ay_r)
    s_g = [
        Gather(s_buf.at[panel], ((0, T), (T, T)), s_s.at[panel], sx_r.at[panel], sy_r.at[panel])
        for panel in range(NP)
    ]

    def mask_of(flag_rows, index):
        wide = jnp.broadcast_to(flag_rows[index : index + 1, :], (HEAD, T)).astype(BF)
        return jnp.concatenate([wide] * (T // HEAD), axis=0)

    def split(tile, mask):
        return tile * (jnp.ones_like(mask) - mask), tile * mask

    def dense_b(panel):
        def body(r, _):
            block = b_raw.at[r % 2, (r // 2) % 8, r // 16]
            flag_rows = block[0:HEAD, :].astype(F32)
            base = pl.multiple_of(((r % 4) * 8 + r // 4) * 2 * T, 2 * T)
            for i in range(2):
                tile = block[HEAD + 2 * T * panel + T * i : HEAD + 2 * T * panel + T * (i + 1), :]
                left, right = split(tile, mask_of(flag_rows, i * NP + panel))
                rows = pl.ds(base + T * i, T)
                bd[panel, rows, 0:T] = left
                bd[panel, rows, T : 2 * T] = right
            return 0

        lax.fori_loop(0, 32, body, 0)

    def dense_a():
        for owner in range(8):
            def body(owner=owner):
                block = a_raw.at[owner]
                flag_rows = block[0:HEAD, :].astype(F32)
                for panel in range(NP):
                    for i in range(2):
                        tile = block[HEAD + 2 * T * panel + T * i : HEAD + 2 * T * panel + T * (i + 1), :]
                        left, right = split(tile, mask_of(flag_rows, i * NP + panel))
                        lanes = owner * 2 * T
                        a_dense[panel, T * i : T * (i + 1), lanes : lanes + T] = left
                        a_dense[panel, T * i : T * (i + 1), lanes + T : lanes + 2 * T] = right

            body()

    def choose(i, panel, t, left, right):
        pick = jnp.full((T, T), kc[i, panel, t], jnp.int32)
        return jnp.where(pick == 0, left, right)

    def square(panel):
        part[...] = jnp.zeros_like(part)

        def body(group, _):
            rows = pl.ds(pl.multiple_of(group * 2048, 2048), 2048)
            part[...] += jnp.dot(a_dense[group], bd[panel, rows, :], preferred_element_type=F32)
            return 0

        lax.fori_loop(0, NP, body, 0)
        s_buf[panel, me_c] = part[...].astype(BF)

    def square_out(panel):
        for i in range(2):
            value = s_buf[panel, me_c, T * i : T * (i + 1), :].astype(F32)
            for t in range(2):
                sq_v[i, panel, t] = choose(i, panel, t, value[:, 0:T], value[:, T:]).astype(BF)
        pltpu.make_async_copy(sq_v.at[:, panel], sq_hbm.at[:, panel], out_sem.at[0, panel]).start()

    def cube(group, low, high):
        lhs = jnp.concatenate([s_buf[group, owner] for owner in range(8)], axis=1)

        def body(panel, _):
            got = jnp.dot(lhs, bd[panel, group * 2048 : (group + 1) * 2048, :], preferred_element_type=F32)
            if group == 0:
                acc[panel] = got
            else:
                acc[panel] += got
            return 0

        lax.fori_loop(low, high, body, 0)

    def result(panel):
        for i in range(2):
            own = s_buf[panel, me_c, T * i : T * (i + 1), :].astype(F32)
            value = 3.0 * own - 2.0 * acc[panel, T * i : T * (i + 1), :]
            for t in range(2):
                pu_v[i, panel, t] = choose(i, panel, t, value[:, 0:T], value[:, T:]).astype(BF)
        pltpu.make_async_copy(pu_v.at[:, panel], pu_hbm.at[:, panel], out_sem.at[1, panel]).start()

    def complete(panel):
        for e in range(2):
            for way in range(2):
                z_wait(way, panel, 4, e)
                core_send(panel, behind(way, 4), e, half_span(panel, way))
        other = b_raw.at[1 - core, :, :, pl.ds(*span(panel))]
        pltpu.make_async_copy(other, other, core_r.at[panel]).wait()
        dense_b(panel)
        square(panel)
        s_g[panel].send_y(0)
        s_g[panel].send_x()
        square_out(panel)

    def start_panel(panel):
        if panel > 0:
            for way in range(2):
                z_send(way, panel, 1, 0)
            core_send(panel, z, 0, span(panel))
        xh_copy(panel, 1 - xhi).wait_recv()
        for way in range(2):
            z_send(way, panel, 1, 1)
        core_send(panel, z, 1, span(panel))

    def advance(panel, hop):
        for e in range(2):
            for way in range(2):
                z_wait(way, panel, hop - 1, e)
                z_send(way, panel, hop, e)
                core_send(panel, behind(way, hop - 1), e, span(panel))

    xh_copy(0, xhi).start()
    for way in range(2):
        z_send(way, 0, 1, 0)
    a_g.send_x()
    a_g.send_y(0)
    for panel in range(1, NP):
        xh_copy(panel, xhi).start()
    core_send(0, z, 0, span(0))

    for turn in range(14):
        for panel in range(NP):
            hop = turn - 2 * panel + 1
            if hop == 1:
                start_panel(panel)
            elif 2 <= hop <= 4:
                advance(panel, hop)
        if turn == 1:
            a_g.pass_x()
        if turn == 2:
            a_g.pass_y(0)
        if turn == 3:
            a_g.pass_y(1)
        if turn == 4:
            a_g.finish(0)
            a_g.finish(1)
            dense_a()
        for panel in range(NP):
            ready = 2 * panel + 4
            if turn == ready + 1:
                s_g[panel].pass_x()
            if turn == ready + 2:
                s_g[panel].pass_y(0)
                s_g[panel].pass_y(1)
        for panel in range(NP):
            ready = 2 * panel + 4
            if turn == ready:
                complete(panel)
                for group in range(panel - 1):
                    cube(group, panel, panel + 1)
            if turn == ready + 3:
                s_g[panel].finish(0)
                s_g[panel].finish(1)
                cube(panel, 0, min(panel + 2, NP))
    for panel in range(NP):
        result(panel)

    for panel in range(NP):
        sent = b_raw.at[0, 0:7, :, pl.ds(*span(panel))]
        pltpu.make_async_copy(sent, sent, z_s.at[panel]).wait()
        sent = b_raw.at[0, :, :, pl.ds(*span(panel))]
        pltpu.make_async_copy(sent, sent, core_s.at[panel]).wait()
        s_g[panel].drain()
    a_g.drain()
    sent = b_raw.at[0, 0, 0]
    pltpu.make_async_copy(sent, sent, xh_s).wait()
    for panel in range(NP):
        pltpu.make_async_copy(sq_v.at[:, panel], sq_hbm.at[:, panel], out_sem.at[0, panel]).wait()
        pltpu.make_async_copy(pu_v.at[:, panel], pu_hbm.at[:, panel], out_sem.at[1, panel]).wait()


def shards(x_tiles, x_cols, keep_cols):
    dma = pltpu.SemaphoreType.DMA
    out = jax.ShapeDtypeStruct((2, NP, 2, T, T), BF)
    return tuple(
        pl.pallas_call(
            kernel,
            out_shape=(out, out),
            in_specs=[
                pl.BlockSpec(memory_space=pl.ANY),
                pl.BlockSpec(memory_space=pltpu.SMEM),
                pl.BlockSpec(memory_space=pltpu.SMEM),
            ],
            out_specs=(pl.BlockSpec(memory_space=pl.ANY), pl.BlockSpec(memory_space=pl.ANY)),
            scratch_shapes=[
                pltpu.VMEM((2, 8, 2, ROWS, T), BF),
                pltpu.VMEM((NP, 64 * T, 2 * T), BF),
                pltpu.VMEM((8, ROWS, T), BF),
                pltpu.VMEM((NP, 2 * T, 16 * T), BF),
                pltpu.VMEM((NP, 8, 2 * T, 2 * T), BF),
                pltpu.VMEM((NP, 2 * T, 2 * T), F32),
                pltpu.VMEM((2 * T, 2 * T), F32),
                pltpu.VMEM((2, NP, 2, T, T), BF),
                pltpu.VMEM((2, NP, 2, T, T), BF),
                dma((2, NP, 2)),
                dma,
                dma((NP,)),
                dma((NP,)),
                dma((2, NP, 4, 2)),
                dma((NP,)),
                dma((NP,)),
                dma,
                dma,
                dma((2, 2, 3)),
                dma((NP,)),
                dma((NP,)),
                dma((NP, 2, 2, 3)),
                dma((2, NP)),
            ],
            compiler_params=pltpu.CompilerParams(
                collective_id=0, has_side_effects=True, vmem_limit_bytes=60 * 1024 * 1024
            ),
        )(x_tiles, x_cols, keep_cols)
    )


def solution(mesh):
    in_specs = (P("row", "col", None, None, None), P("row", "col", None), P("row", "col", None))
    out_specs = (P("row", "col", None, None, None), P("row", "col", None, None, None))
    return jax.shard_map(shards, mesh=mesh, in_specs=in_specs, out_specs=out_specs, check_vma=False)
```

```python
import functools

import jax
import jax.numpy as jnp
from jax import lax
from jax.experimental import pallas as pl
from jax.experimental.pallas import tpu as pltpu
from jax.sharding import PartitionSpec as P

T = 128
HEAD = 16
ROWS = HEAD + 8 * T
NP = 4
BF = jnp.bfloat16
F32 = jnp.float32


def span(panel):
    return (0, HEAD + 2 * T) if panel == 0 else (HEAD + 2 * T * panel, 2 * T)


def half_span(panel, which):
    first, size = span(panel)
    cut = size - T
    return (first, cut) if which == 0 else (first + cut, T)


A_HALF = ((0, HEAD + 4 * T), (HEAD + 4 * T, 4 * T))


def kernel(
    x_hbm, xc, kc, sq_hbm, pu_hbm,
    b_raw, bd, a_raw, a_dense, s_buf, acc, part, sq_v, pu_v,
    load_sem, xh_s, xh_r, z_s, z_r, core_s, core_r,
    a_s, ax_r, ay_r, s_s, sx_r, sy_r, out_sem,
):
    row = lax.axis_index("row")
    me_c = lax.axis_index("col")
    xhi, z, core = row // 16, (row // 2) % 8, row % 2
    y, xlo = me_c // 2, me_c % 2

    def row_of(a, b, c):
        return (a * 8 + b) * 2 + c

    z_peer = (row_of(xhi, (z + 1) % 8, core), row_of(xhi, (z + 7) % 8, core))
    xh_peer = row_of(1 - xhi, z, core)
    core_peer = row_of(xhi, z, 1 - core)
    y_peer = (((y + 1) % 4) * 2 + xlo, ((y + 3) % 4) * 2 + xlo)
    xl_peer = y * 2 + 1 - xlo

    own_b = b_raw.at[core, z, xhi]
    own_a = a_raw.at[me_c]
    loads = []
    for panel in range(NP):
        for i in range(2):
            rows = pl.ds(HEAD + 2 * T * panel + T * i, T)
            loads.append(pltpu.make_async_copy(x_hbm.at[i, panel, 0], own_b.at[rows], load_sem.at[0, panel, i]))
            loads.append(pltpu.make_async_copy(x_hbm.at[i, panel, 0], own_a.at[rows], load_sem.at[1, panel, i]))
    for copy in loads:
        copy.start()

    line = lax.broadcasted_iota(jnp.int32, (HEAD, T), 0)
    flags = jnp.zeros((HEAD, T), jnp.int32)
    for i in range(2):
        for panel in range(NP):
            flags = jnp.where(line == i * NP + panel, xc[i, panel, 0], flags)
    flags = flags.astype(F32).astype(BF)
    own_b[0:HEAD, :] = flags
    own_a[0:HEAD, :] = flags

    barrier = pltpu.get_barrier_semaphore()
    for peer in (z_peer[0], z_peer[1], xh_peer, core_peer):
        pl.semaphore_signal(barrier, inc=1, device_id={"row": peer}, device_id_type=pl.DeviceIdType.MESH)
    for peer in (y_peer[0], y_peer[1], xl_peer):
        pl.semaphore_signal(barrier, inc=1, device_id={"col": peer}, device_id_type=pl.DeviceIdType.MESH)
    pl.semaphore_wait(barrier, 7)
    for copy in loads:
        copy.wait()

    def remote(ref, send, recv, target):
        return pltpu.make_async_remote_copy(
            src_ref=ref, dst_ref=ref, send_sem=send, recv_sem=recv,
            device_id=target, device_id_type=pl.DeviceIdType.MESH,
        )

    def xh_copy(panel, plane):
        ref = b_raw.at[core, z, plane, pl.ds(*span(panel))]
        return remote(ref, xh_s, xh_r.at[panel], {"row": xh_peer})

    def z_copy(way, panel, hop, e, source):
        plane = xhi if e == 0 else 1 - xhi
        where = span(panel) if hop < 4 else half_span(panel, way)
        ref = b_raw.at[core, source, plane, pl.ds(*where)]
        return remote(ref, z_s.at[panel], z_r.at[way, panel, hop - 1, e], {"row": z_peer[way]})

    def behind(way, count):
        return (z + (8 - count if way == 0 else count)) % 8

    def z_send(way, panel, hop, e):
        z_copy(way, panel, hop, e, behind(way, hop - 1)).start()

    def z_wait(way, panel, hop, e):
        z_copy(way, panel, hop, e, behind(way, hop)).wait_recv()

    def core_send(panel, source, e, where):
        plane = xhi if e == 0 else 1 - xhi
        ref = b_raw.at[core, source, plane, pl.ds(*where)]
        remote(ref, core_s.at[panel], core_r.at[panel], {"row": core_peer}).start()

    def row_copy(buf, owner, where, send, recv, target):
        return remote(buf.at[owner, pl.ds(*where)], send, recv, {"col": target})

    class Gather:
        def __init__(self, buf, halves, send, x_recv, y_recv):
            self.buf, self.halves, self.send = buf, halves, send
            self.x_recv, self.y_recv = x_recv, y_recv
            self.total = halves[0][1] + halves[1][1]

        def owner(self, e, way, count):
            side = (y + (4 - count if way == 0 else count)) % 4
            return side * 2 + (xlo if e == 0 else 1 - xlo)

        def x_copy(self, owner):
            return row_copy(self.buf, owner, (0, self.total), self.send, self.x_recv, xl_peer)

        def y_copy(self, e, way, hop, which, owner):
            slot = which if hop == 1 else 2
            return row_copy(self.buf, owner, self.halves[which], self.send, self.y_recv.at[e, way, slot], y_peer[way])

        def send_y(self, e):
            for order in range(2):
                for way in range(2):
                    which = order if way == 0 else 1 - order
                    self.y_copy(e, way, 1, which, self.owner(e, way, 0)).start()

        def send_x(self):
            self.x_copy(me_c).start()

        def pass_x(self):
            self.x_copy(xl_peer).wait_recv()
            self.send_y(1)

        def pass_y(self, e):
            for way in range(2):
                self.y_copy(e, way, 1, way, self.owner(e, way, 1)).wait_recv()
                self.y_copy(e, way, 2, way, self.owner(e, way, 1)).start()

        def finish(self, e):
            for way in range(2):
                self.y_copy(e, way, 1, 1 - way, self.owner(e, way, 1)).wait_recv()
            for way in range(2):
                self.y_copy(e, way, 2, way, self.owner(e, way, 2)).wait_recv()

        def drain(self):
            done = self.buf.at[0:7]
            pltpu.make_async_copy(done, done, self.send).wait()

    a_g = Gather(a_raw, A_HALF, a_s, ax_r, ay_r)
    s_g = [
        Gather(s_buf.at[panel], ((0, T), (T, T)), s_s.at[panel], sx_r.at[panel], sy_r.at[panel])
        for panel in range(NP)
    ]

    def mask_of(flag_rows, index):
        wide = jnp.broadcast_to(flag_rows[index : index + 1, :], (HEAD, T)).astype(BF)
        return jnp.concatenate([wide] * (T // HEAD), axis=0)

    def split(tile, mask):
        return tile * (jnp.ones_like(mask) - mask), tile * mask

    def dense_b(panel):
        def body(r, _):
            block = b_raw.at[r % 2, (r // 2) % 8, r // 16]
            flag_rows = block[0:HEAD, :].astype(F32)
            base = pl.multiple_of(((r % 4) * 8 + r // 4) * 2 * T, 2 * T)
            for i in range(2):
                tile = block[HEAD + 2 * T * panel + T * i : HEAD + 2 * T * panel + T * (i + 1), :]
                left, right = split(tile, mask_of(flag_rows, i * NP + panel))
                rows = pl.ds(base + T * i, T)
                bd[panel, rows, 0:T] = left
                bd[panel, rows, T : 2 * T] = right
            return 0

        lax.fori_loop(0, 32, body, 0)

    def dense_a():
        for owner in range(8):
            def body(owner=owner):
                block = a_raw.at[owner]
                flag_rows = block[0:HEAD, :].astype(F32)
                for panel in range(NP):
                    for i in range(2):
                        tile = block[HEAD + 2 * T * panel + T * i : HEAD + 2 * T * panel + T * (i + 1), :]
                        left, right = split(tile, mask_of(flag_rows, i * NP + panel))
                        lanes = owner * 2 * T
                        a_dense[panel, T * i : T * (i + 1), lanes : lanes + T] = left
                        a_dense[panel, T * i : T * (i + 1), lanes + T : lanes + 2 * T] = right

            body()

    def choose(i, panel, t, left, right):
        pick = jnp.full((T, T), kc[i, panel, t], jnp.int32)
        return jnp.where(pick == 0, left, right)

    def square(panel):
        part[...] = jnp.zeros_like(part)

        def body(group, _):
            rows = pl.ds(pl.multiple_of(group * 2048, 2048), 2048)
            part[...] += jnp.dot(a_dense[group], bd[panel, rows, :], preferred_element_type=F32)
            return 0

        lax.fori_loop(0, NP, body, 0)
        s_buf[panel, me_c] = part[...].astype(BF)

    def square_out(panel):
        for i in range(2):
            value = s_buf[panel, me_c, T * i : T * (i + 1), :].astype(F32)
            for t in range(2):
                sq_v[i, panel, t] = choose(i, panel, t, value[:, 0:T], value[:, T:]).astype(BF)
        pltpu.make_async_copy(sq_v.at[:, panel], sq_hbm.at[:, panel], out_sem.at[0, panel]).start()

    def cube(group, low, high):
        lhs = jnp.concatenate([s_buf[group, owner] for owner in range(8)], axis=1)

        def body(panel, _):
            got = jnp.dot(lhs, bd[panel, group * 2048 : (group + 1) * 2048, :], preferred_element_type=F32)
            if group == 0:
                acc[panel] = got
            else:
                acc[panel] += got
            return 0

        lax.fori_loop(low, high, body, 0)

    def half_cube(group, e):
        owners = [side * 2 + (xlo if e == 0 else 1 - xlo) for side in range(4)]
        lhs = jnp.concatenate([s_buf[group, owner] for owner in owners], axis=1)
        rows = [pl.ds(pl.multiple_of(group * 2048 + owner * 256, 256), 256) for owner in owners]

        def body(panel, _):
            rhs = jnp.concatenate([bd[panel, where, :] for where in rows], axis=0)
            acc[panel] += jnp.dot(lhs, rhs, preferred_element_type=F32)
            return 0

        lax.fori_loop(0, NP, body, 0)

    def result(panel):
        for i in range(2):
            own = s_buf[panel, me_c, T * i : T * (i + 1), :].astype(F32)
            value = 3.0 * own - 2.0 * acc[panel, T * i : T * (i + 1), :]
            for t in range(2):
                pu_v[i, panel, t] = choose(i, panel, t, value[:, 0:T], value[:, T:]).astype(BF)
        pltpu.make_async_copy(pu_v.at[:, panel], pu_hbm.at[:, panel], out_sem.at[1, panel]).start()

    def complete(panel):
        for e in range(2):
            for way in range(2):
                z_wait(way, panel, 4, e)
                core_send(panel, behind(way, 4), e, half_span(panel, way))
        other = b_raw.at[1 - core, :, :, pl.ds(*span(panel))]
        pltpu.make_async_copy(other, other, core_r.at[panel]).wait()
        dense_b(panel)
        square(panel)
        s_g[panel].send_y(0)
        s_g[panel].send_x()
        square_out(panel)

    def start_panel(panel):
        if panel > 0:
            for way in range(2):
                z_send(way, panel, 1, 0)
            core_send(panel, z, 0, span(panel))
        xh_copy(panel, 1 - xhi).wait_recv()
        for way in range(2):
            z_send(way, panel, 1, 1)
        core_send(panel, z, 1, span(panel))

    def advance(panel, hop):
        for e in range(2):
            for way in range(2):
                z_wait(way, panel, hop - 1, e)
                z_send(way, panel, hop, e)
                core_send(panel, behind(way, hop - 1), e, span(panel))

    xh_copy(0, xhi).start()
    for way in range(2):
        z_send(way, 0, 1, 0)
    a_g.send_x()
    a_g.send_y(0)
    for panel in range(1, NP):
        xh_copy(panel, xhi).start()
    core_send(0, z, 0, span(0))

    for turn in range(11):
        for panel in range(NP):
            hop = turn - panel + 1
            if hop == 1:
                start_panel(panel)
            elif 2 <= hop <= 4:
                advance(panel, hop)
        if turn == 1:
            a_g.pass_x()
        if turn == 2:
            a_g.pass_y(0)
        if turn == 3:
            a_g.pass_y(1)
        if turn == 4:
            a_g.finish(0)
            a_g.finish(1)
            dense_a()
        for panel in range(NP):
            ready = panel + 4
            if turn == ready + 1:
                s_g[panel].pass_x()
            if turn == ready + 2:
                s_g[panel].pass_y(0)
                s_g[panel].pass_y(1)
        for panel in range(NP):
            ready = panel + 4
            if turn == ready:
                complete(panel)
                for group in range(panel - 2):
                    cube(group, panel, panel + 1)
            if turn == ready + 3:
                s_g[panel].finish(0)
                if panel == NP - 1:
                    half_cube(panel, 0)
                    s_g[panel].finish(1)
                    half_cube(panel, 1)
                    continue
                s_g[panel].finish(1)
                cube(panel, 0, min(panel + 3, NP))
    for panel in range(NP):
        result(panel)

    for panel in range(NP):
        sent = b_raw.at[0, 0:7, :, pl.ds(*span(panel))]
        pltpu.make_async_copy(sent, sent, z_s.at[panel]).wait()
        sent = b_raw.at[0, :, :, pl.ds(*span(panel))]
        pltpu.make_async_copy(sent, sent, core_s.at[panel]).wait()
        s_g[panel].drain()
    a_g.drain()
    sent = b_raw.at[0, 0, 0]
    pltpu.make_async_copy(sent, sent, xh_s).wait()
    for panel in range(NP):
        pltpu.make_async_copy(sq_v.at[:, panel], sq_hbm.at[:, panel], out_sem.at[0, panel]).wait()
        pltpu.make_async_copy(pu_v.at[:, panel], pu_hbm.at[:, panel], out_sem.at[1, panel]).wait()


def shards(x_tiles, x_cols, keep_cols):
    dma = pltpu.SemaphoreType.DMA
    out = jax.ShapeDtypeStruct((2, NP, 2, T, T), BF)
    return tuple(
        pl.pallas_call(
            kernel,
            out_shape=(out, out),
            in_specs=[
                pl.BlockSpec(memory_space=pl.ANY),
                pl.BlockSpec(memory_space=pltpu.SMEM),
                pl.BlockSpec(memory_space=pltpu.SMEM),
            ],
            out_specs=(pl.BlockSpec(memory_space=pl.ANY), pl.BlockSpec(memory_space=pl.ANY)),
            scratch_shapes=[
                pltpu.VMEM((2, 8, 2, ROWS, T), BF),
                pltpu.VMEM((NP, 64 * T, 2 * T), BF),
                pltpu.VMEM((8, ROWS, T), BF),
                pltpu.VMEM((NP, 2 * T, 16 * T), BF),
                pltpu.VMEM((NP, 8, 2 * T, 2 * T), BF),
                pltpu.VMEM((NP, 2 * T, 2 * T), F32),
                pltpu.VMEM((2 * T, 2 * T), F32),
                pltpu.VMEM((2, NP, 2, T, T), BF),
                pltpu.VMEM((2, NP, 2, T, T), BF),
                dma((2, NP, 2)),
                dma,
                dma((NP,)),
                dma((NP,)),
                dma((2, NP, 4, 2)),
                dma((NP,)),
                dma((NP,)),
                dma,
                dma,
                dma((2, 2, 3)),
                dma((NP,)),
                dma((NP,)),
                dma((NP, 2, 2, 3)),
                dma((2, NP)),
            ],
            compiler_params=pltpu.CompilerParams(
                collective_id=0, has_side_effects=True, vmem_limit_bytes=60 * 1024 * 1024
            ),
        )(x_tiles, x_cols, keep_cols)
    )


def solution(mesh):
    in_specs = (P("row", "col", None, None, None), P("row", "col", None), P("row", "col", None))
    out_specs = (P("row", "col", None, None, None), P("row", "col", None, None, None))
    return jax.shard_map(shards, mesh=mesh, in_specs=in_specs, out_specs=out_specs, check_vma=False)
```
